32 devices in a mesh: obs: 4 (over z), src: 8 (over y, x, core).
Axes of the slice: x: 2, y: 2, z: 4, core: 2. Of those that a mesh axis runs over, the one named last changes fastest.
Arguments:
- delay_near: bfloat16 [16384, 16384], P('src', 'obs'), may hold values from -0.0625 to 0.0625
- delay_far: bfloat16 [16384, 16384], P('src', 'obs'), may hold values from -0.046875 to 0.046875
- incident: bfloat16 [4, 16384, 192], P(None, 'src'), may hold values from -6 to 6
- current_prev: bfloat16 [16384, 192], P('obs'), may hold values from -0.8984375 to 0.8984375
- current_prev2: bfloat16 [16384, 192], P('obs'), may hold values from -0.8984375 to 0.8984375
Outputs:
- currents: bfloat16 [4, 16384, 192], P(None, 'obs')
The draws below stay inside these ranges and needn't reach their ends.
All inputs are finite; a program needn't handle non-finite values.
Results may differ from the reference program's by a relative error of at most 0.003.
Values may be sent and summed in bfloat16 or wider, within the bound.
No kernel may reach another device: no remote copies, remote signals or barrier semaphores. Data moves between devices by JAX's collectives and lax.ppermute only.
A program may use at most 128 MiB of HBM per device.

```python
import jax
import jax.numpy as jnp

N = 16384
R = 192
STEPS = 4


def spiked(result, key, source, target, parts, factor):
    owner, partner = [(jnp.arange(result.shape[dim]) // (result.shape[dim] // parts)).reshape([-1 if axis == dim else 1 for axis in range(result.ndim)]) for dim in (source, target)]
    chosen = jax.random.permutation(key, parts)[partner]
    strong = (owner == chosen) | (owner == (partner + parts // 2) % parts)
    return jnp.where(strong, factor * result, result)


def shard_levels(stream_key, dims, pieces, low, largest):
    gain = 1.0
    for position, shards_of in pieces:
        steps = jax.random.uniform(jax.random.fold_in(jax.random.fold_in(stream_key, 6), position), (shards_of,), jnp.float32, low / len(pieces), largest / len(pieces))
        gain = gain * jnp.repeat(jnp.exp(steps), dims[position] // shards_of).reshape((-1,) + (1,) * (len(dims) - 1 - position))
    return gain


def centred(rng, shape, scale, reach, shards=(), dtype=jnp.bfloat16):
    result = scale * jax.random.normal(rng, shape, jnp.float32)
    if shards:
        result = result * shard_levels(rng, shape, shards, -0.22, 0.18)
    return jnp.clip(result, -reach, reach).astype(dtype)


def heavy_noise(rng, shape, width, bound, cuts, heavy, kind=jnp.bfloat16):
    values = width * jax.random.normal(rng, shape, jnp.float32)
    if cuts:
        values = values * shard_levels(rng, shape, cuts, -0.22, 0.18)
    return jnp.clip(spiked(values, jax.random.fold_in(rng, 3), *heavy), -bound, bound).astype(kind)


def setup_inputs(seed: int = 0) -> dict:
    arg_keys = jax.random.split(jax.random.key(seed), 6)
    return {
        "delay_near": heavy_noise(arg_keys[0], (N, N), N ** -0.5, 0.0625, ((0, 8), (1, 4)), (1, 0, 8, 2.0)),
        "delay_far": centred(arg_keys[1], (N, N), N ** -0.5, 0.046875, ((0, 8), (1, 4))),
        "incident": centred(arg_keys[2], (STEPS, N, R), 1.0, 6.0, ((1, 8),)),
        "current_prev": jnp.clip(jax.random.uniform(arg_keys[3], (N, R), jnp.float32, -0.8984375, 0.8984375) * shard_levels(arg_keys[3], (N, R), ((0, 4),), -0.4, 0.0), -0.8984375, 0.8984375).astype(jnp.bfloat16),
        "current_prev2": jnp.clip(jax.random.uniform(arg_keys[4], (N, R), jnp.float32, -0.8984375, 0.8984375) * shard_levels(arg_keys[4], (N, R), ((0, 4),), -0.4, 0.0), -0.8984375, 0.8984375).astype(jnp.bfloat16),
    }


def reference(delay_near, delay_far, incident, current_prev, current_prev2):
    lagged = current_prev2
    latest = current_prev
    history = []
    for moment in range(STEPS):
        field_sum = jnp.dot(delay_near, latest, preferred_element_type=jnp.float32)
        field_sum = field_sum + jnp.dot(delay_far, lagged, preferred_element_type=jnp.float32)
        new_current = jnp.tanh(incident[moment].astype(jnp.float32) - field_sum).astype(jnp.bfloat16)
        history.append(new_current)
        lagged = latest
        latest = new_current
    return jnp.stack(history)
```

```python
import jax
import jax.numpy as jnp
from jax import lax
from jax.sharding import PartitionSpec as P

STEPS = 4
STREAMS = 2
AXES = ("obs", "src")


def per_device(delay_near, delay_far, incident, current_prev, current_prev2):
    no, ns = lax.axis_size("obs"), lax.axis_size("src")
    group = ns // no
    rows, width = delay_near.shape
    piece = rows // no
    count = current_prev.shape[1]
    part = count // STREAMS

    scale = 1.0
    while 2 * scale * (width * 0.140625 + 6.0) < 65504.0:
        scale *= 2

    z = lax.axis_index("obs")
    s = lax.axis_index("src")
    owner = s // group

    plane_hops, column_hops = [], []
    for r in range(no):
        plane, column = [], []
        for zz in range(no):
            for ss in range(ns):
                o, c = divmod(ss, group)
                plane.append((zz * ns + ss, zz * ns + no * c + (o ^ zz ^ r)))
                q = ss % no
                column.append((zz * ns + ss, (q ^ zz ^ r) * ns + ss))
        plane_hops.append(plane)
        column_hops.append(column)

    def product(matrix, rhs):
        return lax.dot_general(rhs, matrix, (((1,), (1,)), ((), ())), preferred_element_type=jnp.float32)

    def exchange(partial):
        total = None
        for r in range(no):
            q = owner ^ z ^ r
            part_r = lax.dynamic_slice_in_dim(partial, q * piece, piece, 1)
            got = lax.ppermute(part_r, AXES, plane_hops[r])
            got = lax.ppermute(got, AXES, column_hops[r]).astype(jnp.float32)
            total = got if total is None else total + got
        return total

    def gather(block):
        whole = jnp.zeros((block.shape[0], width), block.dtype)
        chips = [block] + [
            lax.ppermute(block, "src", [(i, i ^ shift) for i in range(ns)]) for shift in range(2, ns, 2)
        ]
        both = []
        for k, got in enumerate(chips):
            both.append((s ^ (2 * k), got))
            other = lax.ppermute(got, "src", [(i, i ^ 1) for i in range(ns)])
            both.append((s ^ (2 * k) ^ 1, other))
        for index, got in both:
            whole = lax.dynamic_update_slice_in_dim(whole, got, index * piece, 1)
        return whole

    latest, lagged, outs = [], [], []
    for k in range(STREAMS):
        cut = slice(k * part, (k + 1) * part)
        latest.append(current_prev[:, cut].T)
        lagged.append(current_prev2[:, cut].T)
        outs.append([])
    far = [product(delay_far, lagged[k]) for k in range(STREAMS)]
    for moment in range(STEPS):
        for k in range(STREAMS):
            cut = slice(k * part, (k + 1) * part)
            field = product(delay_near, latest[k]) + far[k]
            local = incident[moment, :, cut].T.astype(jnp.float32)
            mine = jnp.where(owner == z, local, jnp.zeros_like(local))
            total = exchange(((mine - field) * scale).astype(jnp.float16))
            far[k] = product(delay_far, latest[k])
            law = jnp.tanh(total * (1.0 / scale)).astype(jnp.bfloat16)
            latest[k] = gather(law)
            outs[k].append(latest[k])
    history = jnp.concatenate([jnp.stack(o) for o in outs], axis=1)
    return history.transpose(0, 2, 1)


def solution(mesh):
    in_specs = (
        P("src", "obs"),
        P("src", "obs"),
        P(None, "src", None),
        P("obs", None),
        P("obs", None),
    )
    out_specs = P(None, "obs", None)
    return jax.shard_map(
        per_device, mesh=mesh, in_specs=in_specs, out_specs=out_specs, check_vma=False
    )
```

```python
import jax
import jax.numpy as jnp
from jax import lax
from jax.sharding import PartitionSpec as P

STEPS = 4
STREAMS = 1
AXES = ("obs", "src")


def per_device(delay_near, delay_far, incident, current_prev, current_prev2):
    no, ns = lax.axis_size("obs"), lax.axis_size("src")
    group = ns // no
    rows, width = delay_near.shape
    piece = rows // no
    count = current_prev.shape[1]
    part = count // STREAMS

    scale = 1.0
    while 2 * scale * (width * 0.140625 + 6.0) < 65504.0:
        scale *= 2

    z = lax.axis_index("obs")
    s = lax.axis_index("src")
    owner = s // group

    plane_hops, column_hops = [], []
    for r in range(no):
        plane, column = [], []
        for zz in range(no):
            for ss in range(ns):
                o, c = divmod(ss, group)
                plane.append((zz * ns + ss, zz * ns + group * (o ^ zz ^ r) + c))
                column.append((zz * ns + ss, (o ^ zz ^ r) * ns + ss))
        plane_hops.append(plane)
        column_hops.append(column)

    def product(matrix, rhs):
        return lax.dot_general(rhs, matrix, (((1,), (1,)), ((), ())), preferred_element_type=jnp.float32)

    def exchange(partial):
        total = None
        for r in range(no):
            q = owner ^ z ^ r
            part_r = lax.dynamic_slice_in_dim(partial, q * piece, piece, 1)
            got = lax.ppermute(part_r, AXES, plane_hops[r])
            got = lax.ppermute(got, AXES, column_hops[r]).astype(jnp.float32)
            total = got if total is None else total + got
        return total

    def gather(block):
        whole = jnp.zeros((block.shape[0], width), block.dtype)
        chips = [block] + [
            lax.ppermute(block, "src", [(i, i ^ shift) for i in range(ns)]) for shift in range(2, ns, 2)
        ]
        both = []
        for k, got in enumerate(chips):
            both.append((s ^ (2 * k), got))
            other = lax.ppermute(got, "src", [(i, i ^ 1) for i in range(ns)])
            both.append((s ^ (2 * k) ^ 1, other))
        for index, got in both:
            index = index % group * no + index // group
            whole = lax.dynamic_update_slice_in_dim(whole, got, index * piece, 1)
        return whole

    latest, lagged, outs = [], [], []
    for k in range(STREAMS):
        cut = slice(k * part, (k + 1) * part)
        latest.append(current_prev[:, cut].T)
        lagged.append(current_prev2[:, cut].T)
        outs.append([])
    far = [product(delay_far, lagged[k]) for k in range(STREAMS)]
    for moment in range(STEPS):
        for k in range(STREAMS):
            cut = slice(k * part, (k + 1) * part)
            field = product(delay_near, latest[k]) + far[k]
            local = incident[moment, :, cut].T.astype(jnp.float32)
            mine = jnp.where(owner == z, local, jnp.zeros_like(local))
            total = exchange(((mine - field) * scale).astype(jnp.float16))
            far[k] = product(delay_far, latest[k])
            law = jnp.tanh(total * (1.0 / scale)).astype(jnp.bfloat16)
            latest[k] = gather(law)
            outs[k].append(latest[k])
    history = jnp.concatenate([jnp.stack(o) for o in outs], axis=1)
    return history.transpose(0, 2, 1)


def solution(mesh):
    in_specs = (
        P("src", "obs"),
        P("src", "obs"),
        P(None, "src", None),
        P("obs", None),
        P("obs", None),
    )
    out_specs = P(None, "obs", None)
    return jax.shard_map(
        per_device, mesh=mesh, in_specs=in_specs, out_specs=out_specs, check_vma=False
    )
```

```python
import jax
import jax.numpy as jnp
from jax import lax
from jax.experimental import pallas as pl
from jax.experimental.pallas import tpu as pltpu
from jax.sharding import PartitionSpec as P


STEPS = 4
PARTS = 2
GRANT = 6 << 20
STREAM_GRANT = 36 << 20


def each_strip(rows, body):
    tall = min(rows, 512)

    def step(i, carry):
        body(i, pl.ds(pl.multiple_of(i * tall, tall), tall))
        return carry

    lax.fori_loop(0, rows // tall, step, 0)
    return rows // tall


def columns(place, wide):
    return pl.ds(pl.multiple_of(place * wide, wide), wide)


def table_of(places):
    return jnp.stack([jnp.int32(place) for place in places])


def joined(refs, n):
    parts = [jnp.concatenate([ref[...] for ref in refs[k : k + n]], axis=1) for k in range(0, len(refs), n)]
    return jnp.concatenate(parts, axis=0)


def product(left, rhs):
    return lax.dot_general(left, rhs, (((1,), (1,)), ((), ())), preferred_element_type=jnp.float32).T


def streamed_sum(matrix, blocks, places):
    rows, width = matrix.shape
    n = len(places)
    part, wide = blocks[0].shape
    count = part * len(blocks) // n
    tall = min(rows, 512)

    def kernel(table_ref, matrix_ref, *refs):
        rhs = joined(refs[:-1], n)
        left = jnp.concatenate([matrix_ref[:, columns(table_ref[k], wide)] for k in range(n)], axis=1)
        refs[-1][...] = product(left, rhs)

    return pl.pallas_call(
        kernel,
        grid_spec=pltpu.PrefetchScalarGridSpec(
            num_scalar_prefetch=1,
            grid=(rows // tall,),
            in_specs=[pl.BlockSpec((tall, width), lambda i, table: (i, 0))]
            + [pl.BlockSpec(block.shape, lambda i, table: (0, 0)) for block in blocks],
            out_specs=pl.BlockSpec((count, tall), lambda i, table: (0, i)),
        ),
        out_shape=jax.ShapeDtypeStruct((count, rows), jnp.float32),
        cost_estimate=pl.CostEstimate(
            flops=2 * rows * width * count, bytes_accessed=2 * rows * width, transcendentals=0
        ),
        compiler_params=pltpu.CompilerParams(vmem_limit_bytes=STREAM_GRANT),
    )(table_of(places), matrix, *blocks)


def weighted_sum(matrix, blocks, places, start=None):
    rows = matrix.shape[0]
    n = len(places)
    part, wide = blocks[0].shape
    count = part * len(blocks) // n
    total_blocks = len(blocks)

    def kernel(table_ref, matrix_ref, *refs):
        out = refs[-1]
        rhs = joined(refs[:total_blocks], n)

        def add(i, cut):
            left = jnp.concatenate([matrix_ref[cut, columns(table_ref[k], wide)] for k in range(n)], axis=1)
            total = product(left, rhs)
            if start is not None:
                total = total + refs[total_blocks][:, cut]
            out[:, cut] = total

        each_strip(rows, add)

    operands = [table_of(places), matrix, *blocks] + ([] if start is None else [start])
    vmem = pl.BlockSpec(memory_space=pltpu.VMEM)
    return pl.pallas_call(
        kernel,
        in_specs=[pl.BlockSpec(memory_space=pltpu.SMEM)] + [vmem] * (len(operands) - 1),
        out_specs=vmem,
        out_shape=jax.ShapeDtypeStruct((count, rows), jnp.float32),
        cost_estimate=pl.CostEstimate(
            flops=2 * rows * n * wide * count, bytes_accessed=2 * rows * n * wide, transcendentals=0
        ),
        compiler_params=pltpu.CompilerParams(vmem_limit_bytes=GRANT),
    )(*operands)


def record(history, moment, blocks, places, width):
    part, wide = blocks[0].shape
    n = len(blocks)
    count = part * n // len(places)

    def kernel(table_ref, *refs):
        out, sems = refs[-2], refs[-1]
        copies = []
        for k in range(n):
            which, place = divmod(k, len(places))
            spot = out.at[moment, pl.ds(which * part, part), columns(table_ref[place], wide)]
            copies.append(pltpu.make_async_copy(refs[k], spot, sems.at[k]))
        for copy in copies:
            copy.start()
        for copy in copies:
            copy.wait()

    in_specs = [pl.BlockSpec(memory_space=pltpu.SMEM)] + [pl.BlockSpec(memory_space=pltpu.VMEM)] * n
    operands = [table_of(places), *blocks]
    aliases = {}
    if history is not None:
        in_specs.append(pl.BlockSpec(memory_space=pl.ANY))
        operands.append(history)
        aliases = {n + 1: 0}
    return pl.pallas_call(
        kernel,
        in_specs=in_specs,
        out_specs=pl.BlockSpec(memory_space=pl.ANY),
        out_shape=jax.ShapeDtypeStruct((STEPS, count, width), jnp.bfloat16),
        scratch_shapes=[pltpu.SemaphoreType.DMA((n,))],
        input_output_aliases=aliases,
        cost_estimate=pl.CostEstimate(flops=0, bytes_accessed=4 * count * width, transcendentals=0),
        compiler_params=pltpu.CompilerParams(vmem_limit_bytes=GRANT),
    )(*operands)


def per_device(delay_near, delay_far, incident, current_prev, current_prev2):
    no, ns = lax.axis_size("obs"), lax.axis_size("src")
    group = ns // no
    rows, width = delay_near.shape
    piece = rows // no

    scale = 1.0
    while 2 * scale * (width * 0.140625 + 6.0) < 65504.0:
        scale *= 2

    z = lax.axis_index("obs")
    s = lax.axis_index("src")
    chip, core = s // group, s % group

    def swap(value, axis, shift):
        if shift == 0:
            return value
        size = no if axis == "obs" else ns
        return lax.ppermute(value, axis, [(i, i ^ shift) for i in range(size)])

    def exchange(partial):
        got = []
        for r in range(no):
            block = lax.dynamic_slice_in_dim(partial, (chip ^ r) * piece, piece, 1)
            got.append(swap(block, "src", group * r))
        got = jnp.stack(got)
        total = None
        for r in range(no):
            block = lax.dynamic_index_in_dim(got, chip ^ z ^ r, 0, keepdims=False)
            block = swap(block, "obs", r)
            block = block.astype(jnp.float32)
            total = block if total is None else total + block
        return total

    def gather(block):
        blocks, places = [], []
        for r in range(no):
            got = swap(block, "src", group * r)
            for k in range(group):
                blocks.append(swap(got, "src", k))
                places.append((core ^ k) * no + (chip ^ r))
        if piece % 128:
            whole = jnp.zeros((block.shape[0], width), block.dtype)
            for got, place in zip(blocks, places):
                whole = lax.dynamic_update_slice_in_dim(whole, got, place * piece, 1)
            blocks, places = [whole], [0]
        return blocks, places

    field = streamed_sum(delay_far, [current_prev2.T], [0])
    far = pltpu.with_memory_space_constraint(delay_far, pltpu.VMEM)
    near = pltpu.with_memory_space_constraint(delay_near, pltpu.VMEM)
    field = weighted_sum(near, [current_prev.T], [0], field)
    newer = ([current_prev.T], [0])
    history = None
    part = current_prev.shape[1] // PARTS
    for moment in range(STEPS):
        last = moment + 1 == STEPS
        local = incident[moment].T.astype(jnp.float32)
        mine = jnp.where(chip == z, local, jnp.zeros_like(local))
        partial = ((mine - field) * scale).astype(jnp.float16)
        totals = [exchange(partial[k * part : (k + 1) * part]) for k in range(PARTS)]
        if moment:
            history = record(history, moment - 1, *newer, width)
        if not last:
            field = weighted_sum(far, *newer)
        blocks = []
        for total in totals:
            law = jnp.tanh(total * (1.0 / scale)).astype(jnp.bfloat16)
            got, places = gather(law)
            blocks += got
        newer = (blocks, places)
        if not last:
            field = weighted_sum(near, *newer, field)
    history = record(history, STEPS - 1, *newer, width)
    return history.transpose(0, 2, 1)


def solution(mesh):
    in_specs = (
        P("src", "obs"),
        P("src", "obs"),
        P(None, "src", None),
        P("obs", None),
        P("obs", None),
    )
    out_specs = P(None, "obs", None)
    return jax.shard_map(
        per_device, mesh=mesh, in_specs=in_specs, out_specs=out_specs, check_vma=False
    )
```

```python
import jax
import jax.numpy as jnp
from jax import lax
from jax.experimental import pallas as pl
from jax.experimental.pallas import tpu as pltpu
from jax.sharding import PartitionSpec as P


STEPS = 4
PARTS = 2
GRANT = 6 << 20
STREAM_GRANT = 50 << 20


def each_strip(first, rows, body):
    tall = min(rows, 512)
    number = rows // tall

    def step(i, carry):
        body(pl.ds(pl.multiple_of(first + i * tall, tall), tall), pl.ds(pl.multiple_of(i * tall, tall), tall))
        return carry

    lax.fori_loop(0, number, step, 0, unroll=min(2, number))


def columns(place, wide):
    return pl.ds(pl.multiple_of(place * wide, wide), wide)


def table_of(places):
    return jnp.stack([jnp.int32(place) for place in places])


def joined(refs, n):
    parts = [jnp.concatenate([ref[...] for ref in refs[k : k + n]], axis=1) for k in range(0, len(refs), n)]
    return jnp.concatenate(parts, axis=0)


def product(left, rhs):
    return lax.dot_general(left, rhs, (((1,), (1,)), ((), ())), preferred_element_type=jnp.float32).T


def streamed_sum(pairs):
    rows, width = pairs[0][0].shape
    count = pairs[0][1].shape[0]
    tall = min(rows, 512)
    n = len(pairs)

    def kernel(*refs):
        total = None
        for matrix_ref, block_ref in zip(refs[:n], refs[n:]):
            term = product(matrix_ref[...], block_ref[...])
            total = term if total is None else total + term
        refs[-1][...] = total

    return pl.pallas_call(
        kernel,
        grid=(rows // tall,),
        in_specs=[pl.BlockSpec((tall, width), lambda i: (i, 0))] * n
        + [pl.BlockSpec((count, width), lambda i: (0, 0))] * n,
        out_specs=pl.BlockSpec((count, tall), lambda i: (0, i)),
        out_shape=jax.ShapeDtypeStruct((count, rows), jnp.float32),
        cost_estimate=pl.CostEstimate(
            flops=2 * n * rows * width * count, bytes_accessed=2 * n * rows * width, transcendentals=0
        ),
        compiler_params=pltpu.CompilerParams(vmem_limit_bytes=STREAM_GRANT),
    )(*[matrix for matrix, _ in pairs], *[block for _, block in pairs])


def weighted_sum(matrix, blocks, places, starts=None, span=None):
    first, rows = span or (0, matrix.shape[0])
    n = len(places)
    part, wide = blocks[0].shape
    count = part * len(blocks) // n
    used = len(blocks)
    starts = starts or []
    shares = max(1, len(starts))

    def kernel(table_ref, matrix_ref, *refs):
        out = refs[-1]
        rhs = joined(refs[:used], n)
        for j in range(shares):

            def add(cut, within):
                left = jnp.concatenate([matrix_ref[cut, columns(table_ref[k], wide)] for k in range(n)], axis=1)
                total = product(left, rhs)
                if starts:
                    total = total + refs[used + j][:, within]
                out[:, cut if starts else within] = total

            each_strip(first + j * (rows // shares), rows // shares, add)

    operands = [table_of(places), matrix, *blocks, *starts]
    vmem = pl.BlockSpec(memory_space=pltpu.VMEM)
    return pl.pallas_call(
        kernel,
        in_specs=[pl.BlockSpec(memory_space=pltpu.SMEM)] + [vmem] * (len(operands) - 1),
        out_specs=vmem,
        out_shape=jax.ShapeDtypeStruct((count, rows), jnp.float32),
        cost_estimate=pl.CostEstimate(
            flops=2 * rows * n * wide * count, bytes_accessed=2 * rows * n * wide, transcendentals=0
        ),
        compiler_params=pltpu.CompilerParams(vmem_limit_bytes=GRANT),
    )(*operands)


def record(history, moment, blocks, places, width):
    part, wide = blocks[0].shape
    n = len(blocks)
    count = part * n // len(places)

    def kernel(table_ref, *refs):
        out, sems = refs[-2], refs[-1]
        copies = []
        for k in range(n):
            which, place = divmod(k, len(places))
            spot = out.at[moment, pl.ds(which * part, part), columns(table_ref[place], wide)]
            copies.append(pltpu.make_async_copy(refs[k], spot, sems.at[k]))
        for copy in copies:
            copy.start()
        for copy in copies:
            copy.wait()

    in_specs = [pl.BlockSpec(memory_space=pltpu.SMEM)] + [pl.BlockSpec(memory_space=pltpu.VMEM)] * n
    operands = [table_of(places), *blocks]
    aliases = {}
    if history is not None:
        in_specs.append(pl.BlockSpec(memory_space=pl.ANY))
        operands.append(history)
        aliases = {n + 1: 0}
    return pl.pallas_call(
        kernel,
        in_specs=in_specs,
        out_specs=pl.BlockSpec(memory_space=pl.ANY),
        out_shape=jax.ShapeDtypeStruct((STEPS, count, width), jnp.bfloat16),
        scratch_shapes=[pltpu.SemaphoreType.DMA((n,))],
        input_output_aliases=aliases,
        cost_estimate=pl.CostEstimate(flops=0, bytes_accessed=4 * count * width, transcendentals=0),
        compiler_params=pltpu.CompilerParams(vmem_limit_bytes=GRANT),
    )(*operands)


def per_device(delay_near, delay_far, incident, current_prev, current_prev2):
    no, ns = lax.axis_size("obs"), lax.axis_size("src")
    group = ns // no
    rows, width = delay_near.shape
    piece = rows // no

    scale = 1.0
    while 2 * scale * (width * 0.140625 + 6.0) < 65504.0:
        scale *= 2

    z = lax.axis_index("obs")
    s = lax.axis_index("src")
    chip, core = s // group, s % group

    def swap(value, axis, shift):
        if shift == 0:
            return value
        size = no if axis == "obs" else ns
        return lax.ppermute(value, axis, [(i, i ^ shift) for i in range(size)])

    def exchange(partial):
        got = []
        for r in range(no):
            block = lax.dynamic_slice_in_dim(partial, (chip ^ r) * piece, piece, 1)
            got.append(swap(block, "src", group * r))
        got = jnp.stack(got)
        total = None
        for r in range(no):
            block = lax.dynamic_index_in_dim(got, chip ^ z ^ r, 0, keepdims=False)
            block = swap(block, "obs", r)
            block = block.astype(jnp.float32)
            total = block if total is None else total + block
        return total

    def gather(block):
        blocks, places = [], []
        for r in range(no):
            got = swap(block, "src", group * r)
            for k in range(group):
                blocks.append(swap(got, "src", k))
                places.append((core ^ k) * no + (chip ^ r))
        if piece % 128:
            whole = jnp.zeros((block.shape[0], width), block.dtype)
            for got, place in zip(blocks, places):
                whole = lax.dynamic_update_slice_in_dim(whole, got, place * piece, 1)
            blocks, places = [whole], [0]
        return blocks, places

    field = streamed_sum([(delay_far, current_prev2.T), (delay_near, current_prev.T)])
    far = pltpu.with_memory_space_constraint(delay_far, pltpu.VMEM)
    near = pltpu.with_memory_space_constraint(delay_near, pltpu.VMEM)
    newer = ([current_prev.T], [0])
    history = None
    part = current_prev.shape[1] // PARTS
    for moment in range(STEPS):
        last = moment + 1 == STEPS
        local = incident[moment].T.astype(jnp.float32)
        mine = jnp.where(chip == z, local, jnp.zeros_like(local))
        partial = ((mine - field) * scale).astype(jnp.float16)
        totals = [exchange(partial[k * part : (k + 1) * part]) for k in range(PARTS)]
        if moment:
            history = record(history, moment - 1, *newer, width)
        if not last:
            shares = []
            for k in range(PARTS):
                span = (k * (rows // PARTS), rows // PARTS)
                shares.append(weighted_sum(far, *newer, span=span))
        blocks = []
        for total in totals:
            law = jnp.tanh(total * (1.0 / scale)).astype(jnp.bfloat16)
            got, places = gather(law)
            blocks += got
        newer = (blocks, places)
        if not last:
            field = weighted_sum(near, *newer, shares)
    history = record(history, STEPS - 1, *newer, width)
    return history.transpose(0, 2, 1)


def solution(mesh):
    in_specs = (
        P("src", "obs"),
        P("src", "obs"),
        P(None, "src", None),
        P("obs", None),
        P("obs", None),
    )
    out_specs = P(None, "obs", None)
    return jax.shard_map(
        per_device, mesh=mesh, in_specs=in_specs, out_specs=out_specs, check_vma=False
    )
```
